256 devices in a mesh: row: 32 (over x, z), col: 8 (over y, core).
Axes of the slice: x: 4, y: 4, z: 8, core: 2. Of those that a mesh axis runs over, the one named last changes fastest.
Arguments:
- amplitudes: bfloat16 [1024, 16384], P('row', 'col'), may hold values from -6 to 6
- integrals: bfloat16 [16384, 65536], P('col', 'row'), may hold values from -0.09375 to 0.09375
- tile_irrep: int32 [24], replicated, may hold values from 0 to 3
- product_pairs: int32 [256, 2], P('row'), may hold values from 0 to 23, as said below
- summed_pairs: int32 [64, 2], P('col'), may hold values from 0 to 23, as said below
Outputs:
- residual: bfloat16 [1024, 65536], P('col', 'row')
The draws below stay inside these ranges and needn't reach their ends.
Inputs may be any that keep to these rules, and one draw needn't show every extreme that they name: `product_pairs`: for p < 128, entry p + 128 holds the two tiles of entry p in swapped order; the two tiles of an entry differ; no entry repeats. `summed_pairs`: no entry repeats.
All inputs are finite; a program needn't handle non-finite values.
Results may differ from the reference program's by a relative error of at most 0.001.
Values may be sent and summed in bfloat16 or wider, within the bound.
A program may use at most 192 MiB of HBM per device.

```python
import jax
import jax.numpy as jnp
import numpy as np
from jax import lax

TS = 16
TP = 256
NT = 24
OT = 32
OP = 1024
NPC = 64
NPA = 256


def draw_product_pairs(key, part):
    upper_first, upper_second = np.triu_indices(NT, 1)
    first = jnp.asarray(upper_first, dtype=jnp.int32)
    second = jnp.asarray(upper_second, dtype=jnp.int32)
    order = jax.random.permutation(key, first.shape[0])[:NPA // 2]
    left = first[order]
    right = second[order]
    flipped = jax.random.randint(jax.random.fold_in(key, 7), (NPA // 2,), 0, 2)
    head_first = jnp.where(flipped == 1, right, left)
    head_second = jnp.where(flipped == 1, left, right)
    head = jnp.stack([head_first, head_second], axis=1)
    tail = jnp.stack([head_second, head_first], axis=1)
    return jnp.concatenate([head, tail], axis=0).astype(jnp.int32)


def draw_summed_pairs(key, part):
    order = jax.random.permutation(key, NT * NT)[:NPC].astype(jnp.int32)
    return jnp.stack([order // NT, order % NT], axis=1).astype(jnp.int32)


def place_ends(result, key, low, top_value):
    extent = result.shape
    spot = [jax.random.randint(jax.random.fold_in(key, axis), (), 0, extent[axis]) for axis in range(len(extent))]
    result = result.at[tuple(spot)].set(low)
    longest = extent.index(max(extent))
    spot[longest] = (spot[longest] + 1) % extent[longest]
    return result.at[tuple(spot)].set(top_value)


def block_scale(key, extent, pieces, smallest, high):
    level, own = 1.0, jax.random.fold_in(key, 6)
    for position, parts in pieces:
        heights = jnp.exp(jax.random.uniform(jax.random.fold_in(own, position), (parts,), jnp.float32, smallest / len(pieces), high / len(pieces)))
        level = level * jnp.repeat(heights, extent[position] // parts).reshape([-1 if axis == position else 1 for axis in range(len(extent))])
    return level


def noise(own_key, dims, width, reach, cuts=(), kind=jnp.bfloat16):
    result = jax.random.normal(own_key, dims, jnp.float32) * width
    if len(cuts) > 0:
        result = block_scale(own_key, dims, cuts, -0.22, 0.18) * result
    return jnp.clip(result, min=-reach, max=reach).astype(kind)


def setup_inputs(seed: int = 0) -> dict:
    seeds = jax.random.split(jax.random.key(seed), 6)
    return {
        "amplitudes": noise(seeds[0], (OP, NPC * TP), 1.0, 6.0, ((0, 32), (1, 8))),
        "integrals": noise(seeds[1], (NPC * TP, NPA * TP), (NPC * TP // 4) ** -0.5, 0.09375, ((0, 8), (1, 32))),
        "tile_irrep": place_ends(jax.random.randint(seeds[2], (NT,), 0, 4), jax.random.fold_in(seeds[2], 1), 0, 3).astype(jnp.int32),
        "product_pairs": draw_product_pairs(jax.random.fold_in(seeds[5], 71), 0),
        "summed_pairs": draw_summed_pairs(jax.random.fold_in(seeds[5], 71), 0),
    }


def pair_symmetry(tile_irrep, pairs):
    return jnp.bitwise_xor(tile_irrep[pairs[:, 0]], tile_irrep[pairs[:, 1]])


def reference(amplitudes, integrals, tile_irrep, product_pairs, summed_pairs):
    product_sym = pair_symmetry(tile_irrep, product_pairs)
    summed_sym = pair_symmetry(tile_irrep, summed_pairs)
    allowed = summed_sym[:, None] == product_sym[None, :]

    def one_block(index):
        keep = jnp.repeat(allowed[:, index], TP).astype(amplitudes.dtype)
        masked = amplitudes * keep[None, :]
        panel = lax.dynamic_slice_in_dim(integrals, index * TP, TP, 1)
        return jnp.dot(masked, panel, preferred_element_type=jnp.float32)

    blocks = lax.map(one_block, jnp.arange(NPA, dtype=jnp.int32))
    ladder = jnp.transpose(blocks, (1, 0, 2)).reshape(OT, OT, NPA, TS, TS)
    partner = jnp.roll(ladder, NPA // 2, axis=2)
    partner = jnp.transpose(partner, (1, 0, 2, 4, 3))
    return (ladder + partner).reshape(OT * OT, NPA * TP).astype(jnp.bfloat16)
```

```python
import jax
import jax.numpy as jnp
from jax import lax
from jax.sharding import PartitionSpec as P

TS = 16
OT = 32


def from_partner(value, axis, distance):
    mask = 2**distance
    pairs = [(source, source ^ mask) for source in range(lax.axis_size(axis))]
    return lax.ppermute(value, axis, pairs)


def pair_symmetry(tile_irrep, pairs):
    return jnp.bitwise_xor(tile_irrep[pairs[:, 0]], tile_irrep[pairs[:, 1]])


def on_device(amplitudes, integrals, tile_irrep, product_pairs, summed_pairs):
    product_sym = pair_symmetry(tile_irrep, product_pairs)
    summed_sym = pair_symmetry(tile_irrep, summed_pairs)
    allowed = summed_sym[:, None] == product_sym[None, :]
    summed_count = summed_pairs.shape[0]
    product_count = product_pairs.shape[0]
    pair_size = TS * TS
    keep = allowed.astype(integrals.dtype)
    masked = (
        integrals.reshape(summed_count, pair_size, product_count, pair_size)
        * keep[:, None, :, None]
    ).reshape(integrals.shape)
    half_bit = lax.axis_size("row").bit_length() - 2
    ladder = jnp.dot(
        lax.all_gather(amplitudes, "row", axis=0, tiled=True),
        masked,
        preferred_element_type=jnp.float32,
    )
    ladder = lax.psum_scatter(ladder, "col", scatter_dimension=1, tiled=True)
    partner = from_partner(ladder, "row", half_bit)
    partner = partner.reshape(OT, OT, TS, TS)
    partner = jnp.transpose(partner, (1, 0, 3, 2)).reshape(ladder.shape)
    total = (ladder + partner).astype(jnp.bfloat16)
    return lax.all_to_all(total, "col", split_axis=0, concat_axis=1, tiled=True)


def solution(mesh):
    return jax.shard_map(
        on_device,
        mesh=mesh,
        in_specs=(P("row", "col"), P("col", "row"), P(), P("row", None), P("col", None)),
        out_specs=P("col", "row"),
        check_vma=False,
    )
```

```python
import jax
import jax.numpy as jnp
from jax import lax
from jax.experimental import pallas as pl
from jax.experimental.pallas import tpu as pltpu
from jax.sharding import PartitionSpec as P

NX, NY, NZ, NK = 4, 4, 8, 2
TS = 16
TP = TS * TS
OT = 32
HALF = 1024
TOP = 32767.0
F32 = jnp.float32
BF16 = jnp.bfloat16
I16 = jnp.int16


def encode(value, code_ref, scale_ref):
    top = jnp.maximum(jnp.max(jnp.abs(value), axis=0, keepdims=True), 1e-30)
    code = jnp.round(value * (TOP / top)).astype(jnp.int32)
    code_ref[...] = code.astype(I16)
    scale_ref[...] = jnp.broadcast_to(top * (1.0 / TOP), scale_ref.shape)


def decode(code_ref, scale_ref):
    return code_ref[...].astype(jnp.int32).astype(F32) * scale_ref[0:1, :]


def kernel(
    irrep, ppairs, spairs, amp, integ, out,
    v, a0, a1, psend, pown, precv, scode, sscale, rcode, rscale,
    lad, lcode, lscale, pcode, pscale, lp, res,
    load, vload, z0s, z0r, x1s, x1r, x0s, x0r, x2s, x2r, z1s, z1r,
    cs, cr, rs, rr, rss, rsr, es, er, ess, esr, fs, fr,
):
    row, col = lax.axis_index("row"), lax.axis_index("col")
    x, z, y, k = row // NZ, row % NZ, col // NK, col % NK
    a = (a0, a1)
    chunk = (x, (x + 3) % NX, (x + 1) % NX, (x + 2) % NX)

    def dev(dx=0, dy=0, dz=0, dk=0):
        return {
            "row": ((x + dx) % NX) * NZ + (z + dz) % NZ,
            "col": ((y + dy) % NY) * NK + (k + dk) % NK,
        }

    def rc(src, dst, ss, rsem, device):
        return pltpu.make_async_remote_copy(
            src_ref=src, dst_ref=dst, send_sem=ss, recv_sem=rsem,
            device_id=device, device_id_type=pl.DeviceIdType.MESH,
        )

    own = []
    for h in range(2):
        own.append(pltpu.make_async_copy(amp.at[:, pl.ds(h * HALF, HALF)], a[h].at[x, z], load.at[h]))
        own[h].start()
    for n in range(8):
        pltpu.make_async_copy(integ.at[:, pl.ds(n * TP, TP)], v.at[n], vload.at[n]).start()

    barrier = pltpu.get_barrier_semaphore()
    peers = [dev(dz=1), dev(dz=7), dev(dx=1), dev(dx=3), dev(dx=2)]
    peers += [{"row": row, "col": (col + d) % 8} for d in range(1, 8)]
    for peer in peers:
        pl.semaphore_signal(barrier, inc=1, device_id=peer, device_id_type=pl.DeviceIdType.MESH)
    pl.semaphore_wait(barrier, len(peers))
    for copy in own:
        copy.wait()

    sent = []

    def go(copy):
        copy.start()
        sent.append(copy)

    SIGN = (1, -1)

    def z0(d, s, h, arrived):
        ref = a[h].at[x, (z - SIGN[d] * (s if arrived else s - 1)) % NZ]
        return rc(ref, ref, z0s.at[d, s - 1, h], z0r.at[d, s - 1, h], dev(dz=SIGN[d]))

    def x1(d, s, arrived):
        m = (x - SIGN[d] * (s if arrived else s - 1)) % NX
        ref = a1.at[m, z]
        if s == 2:
            ref = a1.at[m, z, pl.ds(16 * d, 16)]
        return rc(ref, ref, x1s.at[d, s - 1], x1r.at[d, s - 1], dev(dx=SIGN[d]))

    STEP = (0, -1, 1, -2, 2, -3, 3, 4)

    def x0(d, e, arrived):
        ref = a0.at[(x - SIGN[d] * (1 if arrived else 0)) % NX, (z + STEP[e]) % NZ]
        return rc(ref, ref, x0s.at[d, e], x0r.at[d, e], dev(dx=SIGN[d]))

    def x2(e, arrived):
        d = e % 2
        ref = a0.at[(x - SIGN[d] * (2 if arrived else 1)) % NX, (z + STEP[e]) % NZ]
        return rc(ref, ref, x2s.at[e], x2r.at[e], dev(dx=SIGN[d]))

    def z1(t, d, s, arrived):
        ref = a1.at[chunk[t], (z - SIGN[d] * (s if arrived else s - 1)) % NZ]
        if s == 4:
            ref = a1.at[chunk[t], (z - SIGN[d] * (s if arrived else s - 1)) % NZ, pl.ds(16 * d, 16)]
        return rc(ref, ref, z1s.at[t - 1, d, s - 1], z1r.at[t - 1, d, s - 1], dev(dz=SIGN[d]))

    def z1_send(t, s):
        for d in range(2):
            go(z1(t, d, s, False))

    def z1_take(t, s):
        for d in range(2):
            z1(t, d, s, True).wait_recv()

    def mask(first, count):
        @pl.loop(first, first + count)
        def _(n):
            pltpu.make_async_copy(integ.at[:, pl.ds(pl.multiple_of(n * TP, TP), TP)], v.at[n], vload.at[n]).wait()
            psym = irrep[ppairs[n, 0]] ^ irrep[ppairs[n, 1]]

            @pl.loop(0, 8)
            def _(q):
                ssym = irrep[spairs[q, 0]] ^ irrep[spairs[q, 1]]
                keep = jnp.where(psym == ssym, 1.0, 0.0)
                rows = pl.ds(pl.multiple_of(q * TP, TP), TP)
                v[n, rows, :] = v[n, rows, :] * jnp.full((1, TP), keep, F32).astype(BF16)

    def product(t, n):
        left = a0[chunk[t]].reshape(8 * OT, HALF)
        right = a1[chunk[t]].reshape(8 * OT, HALF)
        acc = jnp.dot(left, v[n, 0:HALF, :], preferred_element_type=F32)
        return acc + jnp.dot(right, v[n, HALF : 2 * HALF, :], preferred_element_type=F32)

    def to_core(t, j):
        return rc(psend.at[t, j], precv.at[t, j], cs.at[t, j], cr.at[t, j], dev(dk=1))

    def other_tiles(t):
        @pl.loop(0, NY)
        def _(o):
            j = 3 - o
            psend[t, j] = product(t, ((y + j) % NY) * NK + 1 - k)
            to_core(t, j).start()

    def own_tiles(t):
        @pl.loop(0, NY)
        def _(o):
            j = 3 - o
            pown[j] = product(t, ((y + j) % NY) * NK + k)

    def to_owner(t, j):
        device = {"row": row, "col": ((y + j) % NY) * NK + k}
        return (
            rc(scode.at[t, j], rcode.at[t, j], rs.at[t, j], rr.at[t, j], device),
            rc(sscale.at[t, j], rscale.at[t, j], rss.at[t, j], rsr.at[t, j], device),
        )

    def scatter(t):
        @pl.loop(0, NY - 1)
        def _(o):
            j = 3 - o
            to_core(t, j).wait_recv()
            encode(pown[j] + precv[t, j], scode.at[t, j], sscale.at[t, j])
            for copy in to_owner(t, j):
                copy.start()

        to_core(t, 0).wait_recv()
        lad[pl.ds(pl.multiple_of(chunk[t] * TP, TP), TP), :] = pown[0] + precv[t, 0]

    def to_partner(t):
        m = chunk[t]
        return (
            rc(lcode.at[m], pcode.at[m], es.at[t], er.at[t], dev(dx=2)),
            rc(lscale.at[m], pscale.at[m], ess.at[t], esr.at[t], dev(dx=2)),
        )

    def from_partner(t):
        m = (chunk[t] + 2) % NX
        return (
            rc(lcode.at[m], pcode.at[m], es.at[t], er.at[t], dev(dx=2)),
            rc(lscale.at[m], pscale.at[m], ess.at[t], esr.at[t], dev(dx=2)),
        )

    def finish(t):
        rows = pl.ds(pl.multiple_of(chunk[t] * TP, TP), TP)
        total = lad[rows, :]
        for j in range(1, NY):
            for copy in to_owner(t, j):
                copy.wait_recv()
            total = total + decode(rcode.at[t, j], rscale.at[t, j])
        lad[rows, :] = total
        encode(total, lcode.at[chunk[t]], lscale.at[chunk[t]])
        for copy in to_partner(t):
            go(copy)

    def partner(t):
        for copy in from_partner(t):
            copy.wait_recv()
        m = (chunk[t] + 2) % NX
        u = lax.broadcasted_iota(jnp.int32, (TP, TP), 0)
        w = lax.broadcasted_iota(jnp.int32, (TP, TP), 1)
        swap = jnp.where(w == (u % TS) * TS + u // TS, 1.0, 0.0).astype(F32)
        moved = jnp.dot(
            decode(pcode.at[m], pscale.at[m]), swap, preferred_element_type=F32, precision=lax.Precision.HIGHEST
        )
        for half in range(2):
            lp[half, pl.ds(pl.multiple_of(m * TP, TP), TP), :] = moved[:, half * 128 : half * 128 + 128]

    for d in range(2):
        for h in range(2):
            go(z0(d, 1, h, False))
    for d in range(2):
        go(x1(d, 1, False))
    for d in range(2):
        go(x0(d, 0, False))
    mask(0, 2)
    for s in range(1, 4):
        for d in range(2):
            for h in range(2):
                z0(d, s, h, True).wait_recv()
                if s < 3 or d == h:
                    go(z0(d, s + 1, h, False))
        for e in (2 * s - 1, 2 * s):
            for d in range(2):
                go(x0(d, e, False))
        if s == 1:
            for d in range(2):
                x1(d, 1, True).wait_recv()
                go(x1(d, 2, False))
        mask(2 * s, 2)
    z1_send(1, 1)
    z1_send(2, 1)
    for d in range(2):
        z0(d, 4, d, True).wait_recv()
    for d in range(2):
        go(x0(d, 7, False))

    def x2_pass(first, last):
        for e in range(first, last):
            x0(e % 2, e, True).wait_recv()
            go(x2(e, False))

    x2_pass(0, 4)
    other_tiles(0)
    for t in (1, 2):
        z1_take(t, 1)
        z1_send(t, 2)
    own_tiles(0)
    x2_pass(4, 8)
    for t in (1, 2):
        z1_take(t, 2)
        z1_send(t, 3)
    scatter(0)
    for d in range(2):
        x1(d, 2, True).wait_recv()
    for t in (1, 2):
        z1_take(t, 3)
        z1_send(t, 4)
        if t == 1:
            z1_send(3, 1)
    z1_take(1, 4)
    for e in range(1, 8, 2):
        x0(0, e, True).wait_recv()
    other_tiles(1)
    z1_take(3, 1)
    z1_send(3, 2)
    own_tiles(1)
    z1_take(2, 4)
    scatter(1)
    for e in range(0, 8, 2):
        x0(1, e, True).wait_recv()
    other_tiles(2)
    z1_take(3, 2)
    z1_send(3, 3)
    own_tiles(2)
    finish(0)
    z1_take(3, 3)
    z1_send(3, 4)
    scatter(2)
    z1_take(3, 4)
    for e in range(8):
        x2(e, True).wait_recv()
    other_tiles(3)
    own_tiles(3)
    finish(1)
    scatter(3)
    partner(0)
    finish(2)
    partner(1)
    partner(2)
    finish(3)
    partner(3)

    def to_place(d):
        c = (col + d) % 8
        return rc(
            res.at[c], out.at[:, pl.ds(pl.multiple_of(col * TP, TP), TP)],
            fs.at[d], fr.at[d], {"row": row, "col": c},
        )

    def arrived(d):
        c = (col + 8 - d) % 8
        return rc(
            res.at[c], out.at[:, pl.ds(pl.multiple_of(c * TP, TP), TP)],
            fs.at[d], fr.at[d], {"row": row, "col": (col + d) % 8},
        )

    def symmetrize(c):
        for i in range(4):
            at = c * 4 + i
            for half in range(2):
                lanes = slice(half * 128, half * 128 + 128)
                mine = lad[pl.ds(pl.multiple_of(at * OT, OT), OT), lanes]
                theirs = lp[half, pl.ds(at, OT, stride=OT), :]
                res[c, i * OT : (i + 1) * OT, lanes] = (mine + theirs).astype(BF16)

    @pl.loop(1, 8)
    def _(d):
        symmetrize((col + d) % 8)
        to_place(d).start()

    symmetrize(col)
    keep_own = pltpu.make_async_copy(res.at[col], out.at[:, pl.ds(pl.multiple_of(col * TP, TP), TP)], load.at[0])
    keep_own.start()

    for copy in sent:
        copy.wait_send()
    for t in range(NX):

        @pl.loop(0, NY)
        def _(j):
            to_core(t, j).wait_send()

        @pl.loop(1, NY)
        def _(j):
            for copy in to_owner(t, j):
                copy.wait_send()

    keep_own.wait()

    @pl.loop(1, 8)
    def _(d):
        to_place(d).wait_send()
        arrived(d).wait_recv()


def on_device(amplitudes, integrals, tile_irrep, product_pairs, summed_pairs):
    smem = pl.BlockSpec(memory_space=pltpu.SMEM)
    hbm = pl.BlockSpec(memory_space=pl.ANY)
    dma = pltpu.SemaphoreType.DMA
    return pl.pallas_call(
        kernel,
        name="ladder",
        out_shape=jax.ShapeDtypeStruct((128, 2048), BF16),
        in_specs=[smem, smem, smem, hbm, hbm],
        out_specs=pl.BlockSpec(memory_space=pltpu.VMEM),
        scratch_shapes=[
            pltpu.VMEM((8, 2 * HALF, TP), BF16),
            pltpu.VMEM((NX, NZ, OT, HALF), BF16),
            pltpu.VMEM((NX, NZ, OT, HALF), BF16),
            pltpu.VMEM((NX, NY, TP, TP), F32),
            pltpu.VMEM((NY, TP, TP), F32),
            pltpu.VMEM((NX, NY, TP, TP), F32),
            pltpu.VMEM((NX, NY, TP, TP), I16),
            pltpu.VMEM((NX, NY, 8, TP), F32),
            pltpu.VMEM((NX, NY, TP, TP), I16),
            pltpu.VMEM((NX, NY, 8, TP), F32),
            pltpu.VMEM((OT * OT, TP), F32),
            pltpu.VMEM((NX, TP, TP), I16),
            pltpu.VMEM((NX, 8, TP), F32),
            pltpu.VMEM((NX, TP, TP), I16),
            pltpu.VMEM((NX, 8, TP), F32),
            pltpu.VMEM((2, OT * OT, 128), F32),
            pltpu.VMEM((8, 128, TP), BF16),
            dma((2,)), dma((8,)),
            dma((2, 4, 2)), dma((2, 4, 2)),
            dma((2, 2)), dma((2, 2)),
            dma((2, 8)), dma((2, 8)),
            dma((8,)), dma((8,)),
            dma((3, 2, 4)), dma((3, 2, 4)),
            dma((4, 4)), dma((4, 4)),
            dma((4, 4)), dma((4, 4)), dma((4, 4)), dma((4, 4)),
            dma((4,)), dma((4,)), dma((4,)), dma((4,)),
            dma((8,)), dma((8,)),
        ],
        compiler_params=pltpu.CompilerParams(collective_id=0, has_side_effects=True, vmem_limit_bytes=56 << 20),
    )(tile_irrep, product_pairs, summed_pairs, amplitudes, integrals)


def solution(mesh):
    return jax.shard_map(
        on_device,
        mesh=mesh,
        in_specs=(P("row", "col"), P("col", "row"), P(), P("row", None), P("col", None)),
        out_specs=P("col", "row"),
        check_vma=False,
    )
```

```python
import jax
import jax.numpy as jnp
from jax import lax
from jax.experimental import pallas as pl
from jax.experimental.pallas import tpu as pltpu
from jax.sharding import PartitionSpec as P

NX, NY, NZ, NK = 4, 4, 8, 2
TS = 16
TP = TS * TS
OT = 32
HALF = 1152
REST = 2048 - HALF
TOP = 32767.0
F32 = jnp.float32
BF16 = jnp.bfloat16
I16 = jnp.int16


def encode(value, code_ref, scale_ref):
    top = jnp.maximum(jnp.max(jnp.abs(value), axis=0, keepdims=True), 1e-30)
    code_ref[...] = jnp.round(value * (TOP / top)).astype(jnp.int32).astype(I16)
    scale_ref[...] = top * (1.0 / TOP)


def decode(code_ref, scale_ref):
    return code_ref[...].astype(jnp.int32).astype(F32) * scale_ref[...]


STEP = (0, -1, 1, -2, 2, -3, 3, 4)
SLOT = {step % NZ: slot for slot, step in enumerate(STEP)}
GROUPS = ((0,), (1, 2), (3, 4), (5, 6), (7,))
SUB = NX * OT


def kernel(
    irrep, ppairs, spairs, amp, integ, out,
    v, a0, a1, psend, pown, precv, scode, sscale, rcode, rscale, lad,
    gsend, gsendscale, gcode, gscale, qsend, qsendscale, qcode, qscale, turn, acc,
    load, vload, z0s, z0r, x1s, x1r, x0s, x0r, x2s, x2r, z1s, z1r,
    cs, cr, rs, rr, rss, rsr, gs, gr, gss, gsr, qs, qr, qss, qsr,
):
    row, col = lax.axis_index("row"), lax.axis_index("col")
    x, z, y, k = row // NZ, row % NZ, col // NK, col % NK
    a = (a0, a1)
    chunk = (x, (x + 3) % NX, (x + 1) % NX, (x + 2) % NX)
    SIGN = (1, -1)

    def dev(dx=0, dz=0):
        return {"row": ((x + dx) % NX) * NZ + (z + dz) % NZ, "col": col}

    def rc(src, dst, ss, rsem, device):
        return pltpu.make_async_remote_copy(
            src_ref=src, dst_ref=dst, send_sem=ss, recv_sem=rsem,
            device_id=device, device_id_type=pl.DeviceIdType.MESH,
        )

    own = []
    for h in range(2):
        own.append(pltpu.make_async_copy(amp.at[:, pl.ds(h * HALF, (HALF, REST)[h])], a[h].at[0, x], load.at[h]))
        own[h].start()
    for n in range(8):
        pltpu.make_async_copy(integ.at[:, pl.ds(n * TP, TP)], v.at[n], vload.at[n]).start()

    across = ((x + 2) % NX) * NZ + z
    barrier = pltpu.get_barrier_semaphore()
    peers = [dev(dz=1), dev(dz=7), dev(dx=1), dev(dx=3)]
    peers += [{"row": row, "col": (col + d) % 8} for d in range(1, 8)]
    peers += [{"row": across, "col": d} for d in range(8)]
    for peer in peers:
        pl.semaphore_signal(barrier, inc=1, device_id=peer, device_id_type=pl.DeviceIdType.MESH)
    pl.semaphore_wait(barrier, len(peers))
    for copy in own:
        copy.wait()

    def go(copy):
        copy.start()

    def whole(src, dst, ss, rsem):
        return rc(src, dst, ss, rsem, dev(dz=1))

    def z0(d, s, h):
        src, dst = SLOT[-SIGN[d] * (s - 1) % NZ], SLOT[-SIGN[d] * s % NZ]
        return rc(a[h].at[src, x], a[h].at[dst, x], z0s.at[h], z0r.at[s - 1, h], dev(dz=SIGN[d]))

    def x1(d, s, arrived):
        m = (x - SIGN[d] * (s if arrived else s - 1)) % NX
        ref = a1.at[0, m] if s == 1 else a1.at[0, m, pl.ds(16 * d, 16)]
        return rc(ref, ref, x1s.at[0], x1r.at[d, s - 1], dev(dx=SIGN[d]))

    def x0(d, e, arrived):
        ref = a0.at[e, (x - SIGN[d] * (1 if arrived else 0)) % NX]
        return rc(ref, ref, x0s.at[0], x0r.at[d, e], dev(dx=SIGN[d]))

    def x2(e, arrived):
        d = e % 2
        hops = 0 if e == 7 else 1
        ref = a0.at[e, (x - SIGN[d] * (2 if arrived else hops)) % NX]
        return rc(ref, ref, x2s.at[0], x2r.at[e], dev(dx=SIGN[d] * (2 - hops)))

    def z1(t, d, s):
        src, dst = SLOT[-SIGN[d] * (s - 1) % NZ], SLOT[-SIGN[d] * s % NZ]
        m = chunk[t]
        if s == 4:
            part = pl.ds(16 * d, 16)
            src, dst = a1.at[src, m, part], a1.at[dst, m, part]
        else:
            src, dst = a1.at[src, m], a1.at[dst, m]
        return rc(src, dst, z1s.at[0], z1r.at[t - 1, s - 1], dev(dz=SIGN[d]))

    def mask(first, count):
        @pl.loop(first, first + count)
        def _(n):
            pltpu.make_async_copy(integ.at[:, pl.ds(pl.multiple_of(n * TP, TP), TP)], v.at[n], vload.at[n]).wait()
            psym = irrep[ppairs[0, n]] ^ irrep[ppairs[1, n]]

            @pl.loop(0, 8)
            def _(q):
                ssym = irrep[spairs[0, q]] ^ irrep[spairs[1, q]]
                keep = jnp.where(psym == ssym, 1.0, 0.0)
                rows = pl.ds(pl.multiple_of(q * TP, TP), TP)
                v[n, rows, :] = v[n, rows, :] * jnp.full((1, TP), keep, F32).astype(BF16)

    def span(g):
        return pl.ds(GROUPS[g][0] * SUB, len(GROUPS[g]) * SUB)

    def product(g, n):
        size = len(GROUPS[g])
        slots = slice(GROUPS[g][0], GROUPS[g][0] + size)
        left = a0[slots].reshape(size * SUB, HALF)
        right = a1[slots].reshape(size * SUB, REST)
        total = jnp.dot(left, v[n, 0:HALF, :], preferred_element_type=F32)
        return total + jnp.dot(right, v[n, HALF : HALF + REST, :], preferred_element_type=F32)

    def to_core(g, j):
        device = {"row": row, "col": y * NK + 1 - k}
        return rc(psend.at[j, span(g)], precv.at[j, span(g)], cs.at[0], cr.at[g], device)

    def other_tiles(g, first=0, last=NY):
        @pl.loop(first, last)
        def _(o):
            j = 3 - o
            psend[j, span(g), :] = product(g, ((y + j) % NY) * NK + 1 - k)
            to_core(g, j).start()

    def own_tiles(g, first=0, last=NY):
        @pl.loop(first, last)
        def _(o):
            j = 3 - o
            pown[j, 0 : len(GROUPS[g]) * SUB, :] = product(g, ((y + j) % NY) * NK + k)

    def to_owner(g, j):
        device = {"row": row, "col": ((y + j) % NY) * NK + k}
        return (
            rc(scode.at[j, span(g)], rcode.at[j, span(g)], rs.at[0], rr.at[g], device),
            rc(sscale.at[g, j], rscale.at[g, j], rss.at[0], rsr.at[g], device),
        )

    def scatter(g):
        rows = slice(0, len(GROUPS[g]) * SUB)
        whole(psend.at[:, span(g)], precv.at[:, span(g)], cs.at[0], cr.at[g]).wait_recv()

        @pl.loop(0, NY - 1)
        def _(o):
            j = 3 - o
            encode(pown[j, rows, :] + precv[j, span(g), :], scode.at[j, span(g)], sscale.at[g, j])
            for copy in to_owner(g, j):
                copy.start()

        lad[span(g), :] = pown[0, rows, :] + precv[0, span(g), :]

    def direct(e, at):
        zz = (z + STEP[e]) % NZ
        c = at * NK + zz // 4
        rows = pl.ds(pl.multiple_of(at * OT, OT), OT)
        device = {"row": row, "col": c}
        remote = lambda: (
            rc(gsend.at[e, rows], gcode.at[zz % 4, col], gs.at[0], gr.at[zz % 4], device),
            rc(gsendscale.at[e], gscale.at[zz % 4, col], gss.at[0], gsr.at[zz % 4], device),
        )
        local = lambda: (
            pltpu.make_async_copy(gsend.at[e, rows], gcode.at[zz % 4, col], gr.at[zz % 4]),
            pltpu.make_async_copy(gsendscale.at[e], gscale.at[zz % 4, col], gsr.at[zz % 4]),
        )
        return c, remote, local

    def swapped(e, c):
        rows = pl.ds(pl.multiple_of(c * 16, 16), 16)
        device = {"row": across, "col": c}
        return (
            rc(qsend.at[e, rows], qcode.at[e, col], qs.at[0], qr.at[e], device),
            rc(qsendscale.at[e], qscale.at[e, col], qss.at[0], qsr.at[e], device),
        )

    def finish(g):
        total = lad[span(g), :]
        others = pl.ds(1, NY - 1)
        whole(scode.at[others, span(g)], rcode.at[others, span(g)], rs.at[0], rr.at[g]).wait_recv()
        whole(sscale.at[g, others], rscale.at[g, others], rss.at[0], rsr.at[g]).wait_recv()
        for j in range(1, NY):
            total = total + decode(rcode.at[j, span(g)], rscale.at[g, j])
        lad[span(g), :] = total
        u = lax.broadcasted_iota(jnp.int32, (TP, TP), 0)
        w = lax.broadcasted_iota(jnp.int32, (TP, TP), 1)
        swap = jnp.where(w == (u % TS) * TS + u // TS, 1.0, 0.0).astype(F32)
        for e in GROUPS[g]:
            value = lad[e * SUB : (e + 1) * SUB, :]
            moved = jnp.dot(value, swap, preferred_element_type=F32, precision=lax.Precision.HIGHEST)
            for half in range(2):
                lanes = slice(half * 128, half * 128 + 128)
                for xx in range(NX):
                    turn[half, pl.ds(xx, OT, stride=NX), :] = moved[xx * OT : (xx + 1) * OT, lanes]
                encode(turn[half], qsend.at[e, :, pl.ds(half * 128, 128)], qsendscale.at[e, :, pl.ds(half * 128, 128)])

            @pl.loop(0, 8)
            def _(c):
                for copy in swapped(e, c):
                    copy.start()

            encode(value, gsend.at[e], gsendscale.at[e])

            @pl.loop(0, NX)
            def _(at):
                c, remote, local = direct(e, at)

                @pl.when(c != col)
                def _():
                    for copy in remote():
                        copy.start()

                @pl.when(c == col)
                def _():
                    for copy in local():
                        copy.start()

    def absorb(g):
        for e in GROUPS[g]:
            zz = (z + STEP[e]) % NZ
            whole(qcode.at[e], qcode.at[e], qs.at[0], qr.at[e]).wait_recv()
            whole(qscale.at[e], qscale.at[e], qss.at[0], qsr.at[e]).wait_recv()

            @pl.loop(0, 8)
            def _(c):
                value = decode(qcode.at[e, c], qscale.at[e, c])
                for half in range(2):
                    acc[half, c, pl.ds(pl.multiple_of(zz * 16, 16), 16), :] = value[:, half * 128 : half * 128 + 128]

    def take_z0(s, h):
        if s < 4:
            both = a[h].at[pl.ds(2 * s - 1, 2), x]
            whole(both, both, z0s.at[h], z0r.at[s - 1, h]).wait_recv()
            for d in range(2):
                if s < 3 or d == h:
                    go(z0(d, s + 1, h))
        else:
            for d in range(2):
                z0(d, 4, d).wait_recv()
        if h == 0:
            for e in (2 * s - 1, 2 * s):
                if e < 8:
                    for d in range(2):
                        go(x0(d, e, False))
            if s == 4:
                go(x2(7, False))

    def take_x1(s):
        for d in range(2):
            x1(d, s, True).wait_recv()
            if s == 1:
                go(x1(d, 2, False))

    def take_x0(e):
        x0(e % 2, e, True).wait_recv()
        if e < 7:
            go(x2(e, False))

    def take_z1(t, s):
        both = a1.at[7, chunk[t]] if s == 4 else a1.at[pl.ds(2 * s - 1, 2), chunk[t]]
        whole(both, both, z1s.at[0], z1r.at[t - 1, s - 1]).wait_recv()
        if s < 4:
            for d in range(2):
                go(z1(t, d, s + 1))

    def start_z1(t):
        for d in range(2):
            go(z1(t, d, 1))

    def ready(g):
        for e in GROUPS[g]:
            x0(1 - e % 2, e, True).wait_recv()
            x2(e, True).wait_recv()

    for d in range(2):
        go(x1(d, 1, False))
    for d in range(2):
        go(z0(d, 1, 0))
    for d in range(2):
        go(x0(d, 0, False))
    mask(0, 2)
    for d in range(2):
        go(z0(d, 1, 1))
    take_z0(1, 0)
    take_x1(1)
    take_z0(1, 1)
    start_z1(1)
    start_z1(2)
    take_x0(0)
    mask(2, 2)
    take_x1(2)
    start_z1(3)
    mask(4, 2)
    take_z0(2, 0)
    take_z0(2, 1)
    take_z1(1, 1)
    take_z1(2, 1)
    take_x0(1)
    take_x0(2)
    take_z1(3, 1)
    mask(6, 2)
    ready(0)
    other_tiles(0)
    own_tiles(0)
    take_z0(3, 0)
    scatter(0)
    take_x0(3)
    take_x0(4)
    take_z0(3, 1)
    take_z1(1, 2)
    take_z1(2, 2)
    take_z1(3, 2)
    ready(1)
    other_tiles(1)
    take_z0(4, 0)
    own_tiles(1)
    scatter(1)
    take_z1(1, 3)
    take_z1(2, 3)
    take_x0(5)
    take_x0(6)
    take_z1(3, 3)
    ready(2)
    other_tiles(2)
    take_x0(7)
    own_tiles(2)
    scatter(2)
    finish(0)
    take_z1(1, 4)
    take_z1(2, 4)
    take_z1(3, 4)
    ready(3)
    other_tiles(3)
    own_tiles(3)
    scatter(3)
    ready(4)
    other_tiles(4)
    own_tiles(4)
    finish(1)
    scatter(4)
    finish(2)
    absorb(0)
    absorb(1)
    finish(3)
    absorb(2)
    finish(4)
    absorb(3)
    absorb(4)

    for i in range(4):
        whole(gcode.at[i], gcode.at[i], gs.at[0], gr.at[i]).wait_recv()
        whole(gscale.at[i], gscale.at[i], gss.at[0], gsr.at[i]).wait_recv()

    @pl.loop(0, 8)
    def _(c):
        for i in range(4):
            mine = decode(gcode.at[i, c], gscale.at[i, c])
            for half in range(2):
                theirs = jnp.concatenate([acc[half, c, pl.ds(i * 4 + xx, 8, stride=16), :] for xx in range(NX)], axis=0)
                lanes = pl.ds(pl.multiple_of(c * TP + half * 128, 128), 128)
                out[i * OT : (i + 1) * OT, lanes] = (mine[:, half * 128 : half * 128 + 128] + theirs).astype(BF16)

    def left(ref, sem, rsem):
        whole(ref, ref, sem, rsem).wait_send()

    left(a0.at[pl.ds(0, 7), 0], z0s.at[0], z0r.at[0, 0])
    left(a1.at[pl.ds(0, 7), 0], z0s.at[1], z0r.at[0, 1])
    left(a1.at[0, pl.ds(0, 3)], x1s.at[0], x1r.at[0, 0])
    left(a0.at[:, pl.ds(0, 2)], x0s.at[0], x0r.at[0, 0])
    left(a0.at[:, 0], x2s.at[0], x2r.at[0])
    left(a1.at[pl.ds(0, 7), pl.ds(0, 3)], z1s.at[0], z1r.at[0, 0])
    others = pl.ds(1, NY - 1)
    left(psend, cs.at[0], cr.at[0])
    left(scode.at[others], rs.at[0], rr.at[0])
    left(sscale.at[:, others], rss.at[0], rsr.at[0])
    left(gsend.at[pl.ds(0, 7)], gs.at[0], gr.at[0])
    left(gscale.at[:, pl.ds(0, 7)], gss.at[0], gsr.at[0])
    left(qsend, qs.at[0], qr.at[0])
    left(qscale, qss.at[0], qsr.at[0])


def on_device(amplitudes, integrals, tile_irrep, product_pairs, summed_pairs):
    smem = pl.BlockSpec(memory_space=pltpu.SMEM)
    hbm = pl.BlockSpec(memory_space=pl.ANY)
    dma = pltpu.SemaphoreType.DMA
    return pl.pallas_call(
        kernel,
        name="ladder",
        out_shape=jax.ShapeDtypeStruct((128, 2048), BF16),
        in_specs=[smem, smem, smem, hbm, hbm],
        out_specs=pl.BlockSpec(memory_space=pltpu.VMEM),
        scratch_shapes=[
            pltpu.VMEM((8, HALF + REST, TP), BF16),
            pltpu.VMEM((NZ, NX, OT, HALF), BF16),
            pltpu.VMEM((NZ, NX, OT, REST), BF16),
            pltpu.VMEM((NY, OT * OT, TP), F32),
            pltpu.VMEM((NY, 2 * SUB, TP), F32),
            pltpu.VMEM((NY, OT * OT, TP), F32),
            pltpu.VMEM((NY, OT * OT, TP), I16),
            pltpu.VMEM((5, NY, 1, TP), F32),
            pltpu.VMEM((NY, OT * OT, TP), I16),
            pltpu.VMEM((5, NY, 1, TP), F32),
            pltpu.VMEM((OT * OT, TP), F32),
            pltpu.VMEM((8, SUB, TP), I16),
            pltpu.VMEM((8, 1, TP), F32),
            pltpu.VMEM((4, 8, OT, TP), I16),
            pltpu.VMEM((4, 8, 1, TP), F32),
            pltpu.VMEM((8, SUB, TP), I16),
            pltpu.VMEM((8, 1, TP), F32),
            pltpu.VMEM((8, 8, 16, TP), I16),
            pltpu.VMEM((8, 8, 1, TP), F32),
            pltpu.VMEM((2, SUB, 128), F32),
            pltpu.VMEM((2, 8, SUB, 128), F32),
            dma((2,)), dma((8,)),
            dma((2,)), dma((4, 2)),
            dma((1,)), dma((2, 2)),
            dma((1,)), dma((2, 8)),
            dma((1,)), dma((8,)),
            dma((1,)), dma((3, 4)),
            dma((1,)), dma((5,)),
            dma((1,)), dma((5,)), dma((1,)), dma((5,)),
            dma((1,)), dma((4,)), dma((1,)), dma((4,)),
            dma((1,)), dma((8,)), dma((1,)), dma((8,)),
        ],
        compiler_params=pltpu.CompilerParams(collective_id=0, has_side_effects=True, vmem_limit_bytes=56 << 20),
    )(tile_irrep, product_pairs.T, summed_pairs.T, amplitudes, integrals)


def solution(mesh):
    return jax.shard_map(
        on_device,
        mesh=mesh,
        in_specs=(P("row", "col"), P("col", "row"), P(), P("row", None), P("col", None)),
        out_specs=P("col", "row"),
        check_vma=False,
    )
```

```python
import jax
import jax.numpy as jnp
from jax import lax
from jax.experimental import pallas as pl
from jax.experimental.pallas import tpu as pltpu
from jax.sharding import PartitionSpec as P

NX, NY, NZ, NK = 4, 4, 8, 2
TS = 16
TP = TS * TS
OT = 32
HALF = 1152
REST = 2048 - HALF
TOP = 32767.0
F32 = jnp.float32
BF16 = jnp.bfloat16
I16 = jnp.int16


def encode(value, code_ref, scale_ref):
    top = jnp.maximum(jnp.max(jnp.abs(value), axis=0, keepdims=True), 1e-30)
    code_ref[...] = jnp.round(value * (TOP / top)).astype(jnp.int32).astype(I16)
    scale_ref[...] = top * (1.0 / TOP)


def decode(code_ref, scale_ref):
    return code_ref[...].astype(jnp.int32).astype(F32) * scale_ref[...]


STEP = (0, -1, 1, -2, 2, -3, 3, 4)
SLOT = {step % NZ: slot for slot, step in enumerate(STEP)}
GROUPS = ((0,), (1, 2), (3, 4), (5, 6), (7,))
SUB = NX * OT


def kernel(
    irrep, ppairs, spairs, amp, integ, out,
    v, a0, a1, psend, pown, precv, scode, sscale, rcode, rscale, mscale, nscale, lad,
    gsend, gsendscale, gcode, gscale, qsend, qsendscale, qcode, qscale, turn, acc,
    load, vload, z0s, z0r, x1s, x1r, x0s, x0r, x2s, x2r, z1s, z1r,
    cs, cr, rs, rr, rss, rsr, ms, mr, mss, msr, gs, gr, gss, gsr, qs, qr, qss, qsr,
):
    row, col = lax.axis_index("row"), lax.axis_index("col")
    x, z, y, k = row // NZ, row % NZ, col // NK, col % NK
    a = (a0, a1)
    chunk = (x, (x + 3) % NX, (x + 1) % NX, (x + 2) % NX)
    SIGN = (1, -1)

    def dev(dx=0, dz=0):
        return {"row": ((x + dx) % NX) * NZ + (z + dz) % NZ, "col": col}

    def rc(src, dst, ss, rsem, device):
        return pltpu.make_async_remote_copy(
            src_ref=src, dst_ref=dst, send_sem=ss, recv_sem=rsem,
            device_id=device, device_id_type=pl.DeviceIdType.MESH,
        )

    own = []
    for h in range(2):
        own.append(pltpu.make_async_copy(amp.at[:, pl.ds(h * HALF, (HALF, REST)[h])], a[h].at[0, x], load.at[h]))
        own[h].start()
    for n in range(8):
        pltpu.make_async_copy(integ.at[:, pl.ds(n * TP, TP)], v.at[n], vload.at[n]).start()

    across = ((x + 2) % NX) * NZ + z
    barrier = pltpu.get_barrier_semaphore()
    peers = [dev(dz=1), dev(dz=7), dev(dx=1), dev(dx=3)]
    peers += [{"row": row, "col": (col + d) % 8} for d in range(1, 8)]
    peers += [{"row": across, "col": d} for d in range(8)]
    for peer in peers:
        pl.semaphore_signal(barrier, inc=1, device_id=peer, device_id_type=pl.DeviceIdType.MESH)
    pl.semaphore_wait(barrier, len(peers))
    for copy in own:
        copy.wait()

    def go(copy):
        copy.start()

    def whole(src, dst, ss, rsem):
        return rc(src, dst, ss, rsem, dev(dz=1))

    def z0(d, s, h):
        src, dst = SLOT[-SIGN[d] * (s - 1) % NZ], SLOT[-SIGN[d] * s % NZ]
        return rc(a[h].at[src, x], a[h].at[dst, x], z0s.at[h], z0r.at[s - 1, h], dev(dz=SIGN[d]))

    def x1(d, s, arrived):
        m = (x - SIGN[d] * (s if arrived else s - 1)) % NX
        ref = a1.at[0, m] if s == 1 else a1.at[0, m, pl.ds(16 * d, 16)]
        return rc(ref, ref, x1s.at[0], x1r.at[d, s - 1], dev(dx=SIGN[d]))

    def x0(d, e, arrived):
        ref = a0.at[e, (x - SIGN[d] * (1 if arrived else 0)) % NX]
        return rc(ref, ref, x0s.at[0], x0r.at[d, e], dev(dx=SIGN[d]))

    def x2(e, arrived):
        d = e % 2
        hops = 0 if e == 7 else 1
        ref = a0.at[e, (x - SIGN[d] * (2 if arrived else hops)) % NX]
        return rc(ref, ref, x2s.at[0], x2r.at[e], dev(dx=SIGN[d] * (2 - hops)))

    def z1(t, d, s):
        src, dst = SLOT[-SIGN[d] * (s - 1) % NZ], SLOT[-SIGN[d] * s % NZ]
        m = chunk[t]
        if s == 4:
            part = pl.ds(16 * d, 16)
            src, dst = a1.at[src, m, part], a1.at[dst, m, part]
        else:
            src, dst = a1.at[src, m], a1.at[dst, m]
        return rc(src, dst, z1s.at[0], z1r.at[t - 1, s - 1], dev(dz=SIGN[d]))

    def mask(first, count):
        @pl.loop(first, first + count)
        def _(n):
            pltpu.make_async_copy(integ.at[:, pl.ds(pl.multiple_of(n * TP, TP), TP)], v.at[n], vload.at[n]).wait()
            psym = irrep[ppairs[0, n]] ^ irrep[ppairs[1, n]]

            @pl.loop(0, 8)
            def _(q):
                ssym = irrep[spairs[0, q]] ^ irrep[spairs[1, q]]
                keep = jnp.where(psym == ssym, 1.0, 0.0)
                rows = pl.ds(pl.multiple_of(q * TP, TP), TP)
                v[n, rows, :] = v[n, rows, :] * jnp.full((1, TP), keep, F32).astype(BF16)

    def span(g):
        return pl.ds(GROUPS[g][0] * SUB, len(GROUPS[g]) * SUB)

    def product(g, n):
        size = len(GROUPS[g])
        slots = slice(GROUPS[g][0], GROUPS[g][0] + size)
        left = a0[slots].reshape(size * SUB, HALF)
        right = a1[slots].reshape(size * SUB, REST)
        total = jnp.dot(left, v[n, 0:HALF, :], preferred_element_type=F32)
        return total + jnp.dot(right, v[n, HALF : HALF + REST, :], preferred_element_type=F32)

    def to_core(g, j):
        device = {"row": row, "col": y * NK + 1 - k}
        return rc(psend.at[j, span(g)], precv.at[j, span(g)], cs.at[0], cr.at[g], device)

    def other_tiles(g, first=0, last=NY):
        @pl.loop(first, last)
        def _(o):
            j = 3 - o
            psend[j, span(g), :] = product(g, ((y + j) % NY) * NK + 1 - k)
            to_core(g, j).start()

    def own_tiles(g, first=0, last=NY):
        @pl.loop(first, last)
        def _(o):
            j = 3 - o
            pown[j, 0 : len(GROUPS[g]) * SUB, :] = product(g, ((y + j) % NY) * NK + k)

    def ahead(d):
        return {"row": row, "col": ((y + (1, 3)[d]) % NY) * NK + k}

    def part(g, d):
        size = len(GROUPS[g]) * SUB // 2
        return pl.ds(GROUPS[g][0] * SUB + d * size, size)

    def to_relay(g, d):
        return (
            rc(scode.at[2, part(g, d)], rcode.at[2, part(g, d)], ms.at[0], mr.at[g], ahead(d)),
            rc(mscale.at[g, d], nscale.at[g, d], mss.at[0], msr.at[g], ahead(d)),
        )

    def to_owner(g, d):
        return (
            rc(scode.at[d, span(g)], rcode.at[d, span(g)], rs.at[0], rr.at[g], ahead(d)),
            rc(sscale.at[g, d], rscale.at[g, d], rss.at[0], rsr.at[g], ahead(d)),
        )

    def scatter(g):
        size = len(GROUPS[g]) * SUB
        whole(psend.at[:, span(g)], precv.at[:, span(g)], cs.at[0], cr.at[g]).wait_recv()
        for d in range(2):
            mine = pown[2, d * size // 2 : (d + 1) * size // 2, :]
            encode(mine + precv[2, part(g, d), :], scode.at[2, part(g, d)], mscale.at[g, d])
            for copy in to_relay(g, d):
                copy.start()
        for j in (1, 3):
            precv[j, span(g), :] = pown[j, 0:size, :] + precv[j, span(g), :]
        lad[span(g), :] = pown[0, 0:size, :] + precv[0, span(g), :]

    def relay(g):
        whole(scode.at[2, span(g)], rcode.at[2, span(g)], ms.at[0], mr.at[g]).wait_recv()
        whole(mscale.at[g], nscale.at[g], mss.at[0], msr.at[g]).wait_recv()
        for d in range(2):
            j = (1, 3)[d]
            precv[j, part(g, d), :] = precv[j, part(g, d), :] + decode(rcode.at[2, part(g, d)], nscale.at[g, d])
            encode(precv[j, span(g), :], scode.at[d, span(g)], sscale.at[g, d])
            for copy in to_owner(g, d):
                copy.start()

    def direct(e, at):
        zz = (z + STEP[e]) % NZ
        c = at * NK + zz // 4
        rows = pl.ds(pl.multiple_of(at * OT, OT), OT)
        device = {"row": row, "col": c}
        remote = lambda: (
            rc(gsend.at[e, rows], gcode.at[zz % 4, col], gs.at[0], gr.at[zz % 4], device),
            rc(gsendscale.at[e], gscale.at[zz % 4, col], gss.at[0], gsr.at[zz % 4], device),
        )
        local = lambda: (
            pltpu.make_async_copy(gsend.at[e, rows], gcode.at[zz % 4, col], gr.at[zz % 4]),
            pltpu.make_async_copy(gsendscale.at[e], gscale.at[zz % 4, col], gsr.at[zz % 4]),
        )
        return c, remote, local

    def swapped(e, c):
        rows = pl.ds(pl.multiple_of(c * 16, 16), 16)
        device = {"row": across, "col": c}
        return (
            rc(qsend.at[e, rows], qcode.at[e, col], qs.at[0], qr.at[e], device),
            rc(qsendscale.at[e], qscale.at[e, col], qss.at[0], qsr.at[e], device),
        )

    def finish(g):
        total = lad[span(g), :]
        others = pl.ds(0, 2)
        whole(scode.at[others, span(g)], rcode.at[others, span(g)], rs.at[0], rr.at[g]).wait_recv()
        whole(sscale.at[g, others], rscale.at[g, others], rss.at[0], rsr.at[g]).wait_recv()
        for j in range(2):
            total = total + decode(rcode.at[j, span(g)], rscale.at[g, j])
        lad[span(g), :] = total
        u = lax.broadcasted_iota(jnp.int32, (TP, TP), 0)
        w = lax.broadcasted_iota(jnp.int32, (TP, TP), 1)
        swap = jnp.where(w == (u % TS) * TS + u // TS, 1.0, 0.0).astype(F32)
        for e in GROUPS[g]:
            value = lad[e * SUB : (e + 1) * SUB, :]
            moved = jnp.dot(value, swap, preferred_element_type=F32, precision=lax.Precision.HIGHEST)
            for half in range(2):
                lanes = slice(half * 128, half * 128 + 128)
                for xx in range(NX):
                    turn[half, pl.ds(xx, OT, stride=NX), :] = moved[xx * OT : (xx + 1) * OT, lanes]
                encode(turn[half], qsend.at[e, :, pl.ds(half * 128, 128)], qsendscale.at[e, :, pl.ds(half * 128, 128)])

            @pl.loop(0, 8)
            def _(c):
                for copy in swapped(e, c):
                    copy.start()

            encode(value, gsend.at[e], gsendscale.at[e])

            @pl.loop(0, NX)
            def _(at):
                c, remote, local = direct(e, at)

                @pl.when(c != col)
                def _():
                    for copy in remote():
                        copy.start()

                @pl.when(c == col)
                def _():
                    for copy in local():
                        copy.start()

    def absorb(g):
        for e in GROUPS[g]:
            zz = (z + STEP[e]) % NZ
            whole(qcode.at[e], qcode.at[e], qs.at[0], qr.at[e]).wait_recv()
            whole(qscale.at[e], qscale.at[e], qss.at[0], qsr.at[e]).wait_recv()

            @pl.loop(0, 8)
            def _(c):
                value = decode(qcode.at[e, c], qscale.at[e, c])
                for half in range(2):
                    acc[half, c, pl.ds(pl.multiple_of(zz * 16, 16), 16), :] = value[:, half * 128 : half * 128 + 128]

    def take_z0(s, h):
        if s < 4:
            both = a[h].at[pl.ds(2 * s - 1, 2), x]
            whole(both, both, z0s.at[h], z0r.at[s - 1, h]).wait_recv()
            for d in range(2):
                if s < 3 or d == h:
                    go(z0(d, s + 1, h))
        else:
            for d in range(2):
                z0(d, 4, d).wait_recv()
        if h == 0:
            for e in (2 * s - 1, 2 * s):
                if e < 8:
                    for d in range(2):
                        go(x0(d, e, False))
            if s == 4:
                go(x2(7, False))

    def take_x1(s):
        for d in range(2):
            x1(d, s, True).wait_recv()
            if s == 1:
                go(x1(d, 2, False))

    def take_x0(e):
        x0(e % 2, e, True).wait_recv()
        if e < 7:
            go(x2(e, False))

    def take_z1(t, s):
        both = a1.at[7, chunk[t]] if s == 4 else a1.at[pl.ds(2 * s - 1, 2), chunk[t]]
        whole(both, both, z1s.at[0], z1r.at[t - 1, s - 1]).wait_recv()
        if s < 4:
            for d in range(2):
                go(z1(t, d, s + 1))

    def start_z1(t):
        for d in range(2):
            go(z1(t, d, 1))

    def ready(g):
        for e in GROUPS[g]:
            x0(1 - e % 2, e, True).wait_recv()
            x2(e, True).wait_recv()

    for d in range(2):
        go(x1(d, 1, False))
    for d in range(2):
        go(z0(d, 1, 0))
    for d in range(2):
        go(x0(d, 0, False))
    mask(0, 2)
    for d in range(2):
        go(z0(d, 1, 1))
    take_z0(1, 0)
    take_x1(1)
    take_z0(1, 1)
    start_z1(1)
    start_z1(2)
    take_x0(0)
    mask(2, 2)
    take_x1(2)
    start_z1(3)
    mask(4, 2)
    take_z0(2, 0)
    take_z0(2, 1)
    take_z1(1, 1)
    take_z1(2, 1)
    take_x0(1)
    take_x0(2)
    take_z1(3, 1)
    mask(6, 2)
    ready(0)
    other_tiles(0)
    own_tiles(0)
    take_z0(3, 0)
    scatter(0)
    take_x0(3)
    take_x0(4)
    take_z0(3, 1)
    take_z1(1, 2)
    take_z1(2, 2)
    take_z1(3, 2)
    ready(1)
    other_tiles(1)
    take_z0(4, 0)
    own_tiles(1)
    relay(0)
    scatter(1)
    take_z1(1, 3)
    take_z1(2, 3)
    take_x0(5)
    take_x0(6)
    take_z1(3, 3)
    ready(2)
    other_tiles(2)
    take_x0(7)
    own_tiles(2)
    scatter(2)
    relay(1)
    take_z1(1, 4)
    take_z1(2, 4)
    take_z1(3, 4)
    ready(3)
    other_tiles(3)
    own_tiles(3)
    scatter(3)
    relay(2)
    ready(4)
    other_tiles(4)
    own_tiles(4)
    scatter(4)
    relay(3)
    finish(0)
    relay(4)
    finish(1)
    finish(2)
    absorb(0)
    finish(3)
    absorb(1)
    finish(4)
    absorb(2)
    absorb(3)
    absorb(4)

    for i in range(4):
        whole(gcode.at[i], gcode.at[i], gs.at[0], gr.at[i]).wait_recv()
        whole(gscale.at[i], gscale.at[i], gss.at[0], gsr.at[i]).wait_recv()

    @pl.loop(0, 8)
    def _(c):
        for i in range(4):
            mine = decode(gcode.at[i, c], gscale.at[i, c])
            for half in range(2):
                theirs = jnp.concatenate([acc[half, c, pl.ds(i * 4 + xx, 8, stride=16), :] for xx in range(NX)], axis=0)
                lanes = pl.ds(pl.multiple_of(c * TP + half * 128, 128), 128)
                out[i * OT : (i + 1) * OT, lanes] = (mine[:, half * 128 : half * 128 + 128] + theirs).astype(BF16)

    def left(ref, sem, rsem):
        whole(ref, ref, sem, rsem).wait_send()

    left(a0.at[pl.ds(0, 7), 0], z0s.at[0], z0r.at[0, 0])
    left(a1.at[pl.ds(0, 7), 0], z0s.at[1], z0r.at[0, 1])
    left(a1.at[0, pl.ds(0, 3)], x1s.at[0], x1r.at[0, 0])
    left(a0.at[:, pl.ds(0, 2)], x0s.at[0], x0r.at[0, 0])
    left(a0.at[:, 0], x2s.at[0], x2r.at[0])
    left(a1.at[pl.ds(0, 7), pl.ds(0, 3)], z1s.at[0], z1r.at[0, 0])
    others = pl.ds(0, 2)
    left(psend, cs.at[0], cr.at[0])
    left(scode.at[others], rs.at[0], rr.at[0])
    left(sscale.at[:, others], rss.at[0], rsr.at[0])
    left(scode.at[2], ms.at[0], mr.at[0])
    left(mscale, mss.at[0], msr.at[0])
    left(gsend.at[pl.ds(0, 7)], gs.at[0], gr.at[0])
    left(gscale.at[:, pl.ds(0, 7)], gss.at[0], gsr.at[0])
    left(qsend, qs.at[0], qr.at[0])
    left(qscale, qss.at[0], qsr.at[0])


def on_device(amplitudes, integrals, tile_irrep, product_pairs, summed_pairs):
    smem = pl.BlockSpec(memory_space=pltpu.SMEM)
    hbm = pl.BlockSpec(memory_space=pl.ANY)
    dma = pltpu.SemaphoreType.DMA
    return pl.pallas_call(
        kernel,
        name="ladder",
        out_shape=jax.ShapeDtypeStruct((128, 2048), BF16),
        in_specs=[smem, smem, smem, hbm, hbm],
        out_specs=pl.BlockSpec(memory_space=pltpu.VMEM),
        scratch_shapes=[
            pltpu.VMEM((8, HALF + REST, TP), BF16),
            pltpu.VMEM((NZ, NX, OT, HALF), BF16),
            pltpu.VMEM((NZ, NX, OT, REST), BF16),
            pltpu.VMEM((NY, OT * OT, TP), F32),
            pltpu.VMEM((NY, 2 * SUB, TP), F32),
            pltpu.VMEM((NY, OT * OT, TP), F32),
            pltpu.VMEM((NY, OT * OT, TP), I16),
            pltpu.VMEM((5, NY, 1, TP), F32),
            pltpu.VMEM((NY, OT * OT, TP), I16),
            pltpu.VMEM((5, NY, 1, TP), F32),
            pltpu.VMEM((5, 2, 1, TP), F32),
            pltpu.VMEM((5, 2, 1, TP), F32),
            pltpu.VMEM((OT * OT, TP), F32),
            pltpu.VMEM((8, SUB, TP), I16),
            pltpu.VMEM((8, 1, TP), F32),
            pltpu.VMEM((4, 8, OT, TP), I16),
            pltpu.VMEM((4, 8, 1, TP), F32),
            pltpu.VMEM((8, SUB, TP), I16),
            pltpu.VMEM((8, 1, TP), F32),
            pltpu.VMEM((8, 8, 16, TP), I16),
            pltpu.VMEM((8, 8, 1, TP), F32),
            pltpu.VMEM((2, SUB, 128), F32),
            pltpu.VMEM((2, 8, SUB, 128), F32),
            dma((2,)), dma((8,)),
            dma((2,)), dma((4, 2)),
            dma((1,)), dma((2, 2)),
            dma((1,)), dma((2, 8)),
            dma((1,)), dma((8,)),
            dma((1,)), dma((3, 4)),
            dma((1,)), dma((5,)),
            dma((1,)), dma((5,)), dma((1,)), dma((5,)),
            dma((1,)), dma((5,)), dma((1,)), dma((5,)),
            dma((1,)), dma((4,)), dma((1,)), dma((4,)),
            dma((1,)), dma((8,)), dma((1,)), dma((8,)),
        ],
        compiler_params=pltpu.CompilerParams(collective_id=0, has_side_effects=True, vmem_limit_bytes=56 << 20),
    )(tile_irrep, product_pairs.T, summed_pairs.T, amplitudes, integrals)


def solution(mesh):
    return jax.shard_map(
        on_device,
        mesh=mesh,
        in_specs=(P("row", "col"), P("col", "row"), P(), P("row", None), P("col", None)),
        out_specs=P("col", "row"),
        check_vma=False,
    )
```

```python
import jax
import jax.numpy as jnp
from jax import lax
from jax.experimental import pallas as pl
from jax.experimental.pallas import tpu as pltpu
from jax.sharding import PartitionSpec as P

NX, NY, NZ, NK = 4, 4, 8, 2
TS = 16
TP = TS * TS
OT = 32
HALF = 1152
REST = 2048 - HALF
TOP = 32767.0
F32 = jnp.float32
BF16 = jnp.bfloat16
I16 = jnp.int16


def encode(value, code_ref, scale_ref):
    top = jnp.maximum(jnp.max(jnp.abs(value), axis=0, keepdims=True), 1e-30)
    code_ref[...] = jnp.round(value * (TOP / top)).astype(jnp.int32).astype(I16)
    scale_ref[...] = top * (1.0 / TOP)


def decode(code_ref, scale_ref):
    return code_ref[...].astype(jnp.int32).astype(F32) * scale_ref[...]


STEP = (0, -1, 1, -2, 2, -3, 3, 4)
SLOT = {step % NZ: slot for slot, step in enumerate(STEP)}
GROUPS = ((0,), (1, 2), (3, 4), (5, 6), (7,))
SUB = NX * OT


def kernel(
    irrep, ppairs, spairs, amp, integ, out,
    v, a0, a1, psend, pown, precv, scode, sscale, rcode, rscale, mscale, nscale, lad,
    gsend, gsendscale, gcode, gscale, qsend, qsendscale, qcode, qscale, turn, acc,
    load, vload, z0s, z0r, x1s, x1r, x0s, x0r, x2s, x2r, z1s, z1r,
    cs, cr, rs, rr, rss, rsr, ms, mr, mss, msr, gs, gr, gss, gsr, qs, qr, qss, qsr,
):
    row, col = lax.axis_index("row"), lax.axis_index("col")
    x, z, y, k = row // NZ, row % NZ, col // NK, col % NK
    a = (a0, a1)
    chunk = (x, (x + 3) % NX, (x + 1) % NX, (x + 2) % NX)
    SIGN = (1, -1)

    def dev(dx=0, dz=0):
        return {"row": ((x + dx) % NX) * NZ + (z + dz) % NZ, "col": col}

    def rc(src, dst, ss, rsem, device):
        return pltpu.make_async_remote_copy(
            src_ref=src, dst_ref=dst, send_sem=ss, recv_sem=rsem,
            device_id=device, device_id_type=pl.DeviceIdType.MESH,
        )

    own = []
    for h in range(2):
        own.append(pltpu.make_async_copy(amp.at[:, pl.ds(h * HALF, (HALF, REST)[h])], a[h].at[0, x], load.at[h]))
        own[h].start()
    for n in range(8):
        pltpu.make_async_copy(integ.at[:, pl.ds(n * TP, TP)], v.at[n], vload.at[n]).start()

    across = ((x + 2) % NX) * NZ + z
    barrier = pltpu.get_barrier_semaphore()
    peers = [dev(dz=1), dev(dz=7), dev(dx=1), dev(dx=3)]
    peers += [{"row": row, "col": (col + d) % 8} for d in range(1, 8)]
    peers += [{"row": across, "col": d} for d in range(8)]
    for peer in peers:
        pl.semaphore_signal(barrier, inc=1, device_id=peer, device_id_type=pl.DeviceIdType.MESH)
    pl.semaphore_wait(barrier, len(peers))
    for copy in own:
        copy.wait()

    def go(copy):
        copy.start()

    def whole(src, dst, ss, rsem):
        return rc(src, dst, ss, rsem, dev(dz=1))

    def z0(d, s, h):
        src, dst = SLOT[-SIGN[d] * (s - 1) % NZ], SLOT[-SIGN[d] * s % NZ]
        return rc(a[h].at[src, x], a[h].at[dst, x], z0s.at[h], z0r.at[s - 1, h], dev(dz=SIGN[d]))

    def x1(d, s, arrived):
        m = (x - SIGN[d] * (s if arrived else s - 1)) % NX
        ref = a1.at[0, m] if s == 1 else a1.at[0, m, pl.ds(16 * d, 16)]
        return rc(ref, ref, x1s.at[0], x1r.at[d, s - 1], dev(dx=SIGN[d]))

    def x0(d, e, arrived):
        ref = a0.at[e, (x - SIGN[d] * (1 if arrived else 0)) % NX]
        return rc(ref, ref, x0s.at[0], x0r.at[d, e], dev(dx=SIGN[d]))

    def x2(e, arrived):
        d = e % 2
        hops = 0 if e == 7 else 1
        ref = a0.at[e, (x - SIGN[d] * (2 if arrived else hops)) % NX]
        return rc(ref, ref, x2s.at[0], x2r.at[e], dev(dx=SIGN[d] * (2 - hops)))

    def z1(t, d, s):
        src, dst = SLOT[-SIGN[d] * (s - 1) % NZ], SLOT[-SIGN[d] * s % NZ]
        m = chunk[t]
        if s == 4:
            part = pl.ds(16 * d, 16)
            src, dst = a1.at[src, m, part], a1.at[dst, m, part]
        else:
            src, dst = a1.at[src, m], a1.at[dst, m]
        return rc(src, dst, z1s.at[0], z1r.at[t - 1, s - 1], dev(dz=SIGN[d]))

    def mask(first, count):
        @pl.loop(first, first + count)
        def _(n):
            pltpu.make_async_copy(integ.at[:, pl.ds(pl.multiple_of(n * TP, TP), TP)], v.at[n], vload.at[n]).wait()
            psym = irrep[ppairs[0, n]] ^ irrep[ppairs[1, n]]

            @pl.loop(0, 8)
            def _(q):
                ssym = irrep[spairs[0, q]] ^ irrep[spairs[1, q]]
                keep = jnp.where(psym == ssym, 1.0, 0.0)
                rows = pl.ds(pl.multiple_of(q * TP, TP), TP)
                v[n, rows, :] = v[n, rows, :] * jnp.full((1, TP), keep, F32).astype(BF16)

    def span(g):
        return pl.ds(GROUPS[g][0] * SUB, len(GROUPS[g]) * SUB)

    def product(g, n):
        size = len(GROUPS[g])
        slots = slice(GROUPS[g][0], GROUPS[g][0] + size)
        left = a0[slots].reshape(size * SUB, HALF)
        right = a1[slots].reshape(size * SUB, REST)
        total = jnp.dot(left, v[n, 0:HALF, :], preferred_element_type=F32)
        return total + jnp.dot(right, v[n, HALF : HALF + REST, :], preferred_element_type=F32)

    def to_core(g, j):
        device = {"row": row, "col": y * NK + 1 - k}
        return rc(psend.at[j, span(g)], precv.at[j, span(g)], cs.at[0], cr.at[g], device)

    def other_tiles(g, first=0, last=NY):
        @pl.loop(first, last)
        def _(o):
            j = 3 - o
            psend[j, span(g), :] = product(g, ((y + j) % NY) * NK + 1 - k)
            to_core(g, j).start()

    def own_tiles(g, first=0, last=NY):
        @pl.loop(first, last)
        def _(o):
            j = 3 - o
            pown[j, 0 : len(GROUPS[g]) * SUB, :] = product(g, ((y + j) % NY) * NK + k)

    def ahead(d):
        return {"row": row, "col": ((y + (1, 3)[d]) % NY) * NK + k}

    def part(g, d):
        size = len(GROUPS[g]) * SUB // 2
        return pl.ds(GROUPS[g][0] * SUB + d * size, size)

    def to_relay(g, d):
        return (
            rc(scode.at[2, part(g, d)], rcode.at[2, part(g, d)], ms.at[0], mr.at[g], ahead(d)),
            rc(mscale.at[g, d], nscale.at[g, d], mss.at[0], msr.at[g], ahead(d)),
        )

    def to_owner(g, d, p):
        return (
            rc(scode.at[d, part(g, p)], rcode.at[d, part(g, p)], rs.at[0], rr.at[g], ahead(d)),
            rc(sscale.at[g, 2 * d + p], rscale.at[g, 2 * d + p], rss.at[0], rsr.at[g], ahead(d)),
        )

    def scatter(g):
        size = len(GROUPS[g]) * SUB
        whole(psend.at[:, span(g)], precv.at[:, span(g)], cs.at[0], cr.at[g]).wait_recv()
        for d in range(2):
            mine = pown[2, d * size // 2 : (d + 1) * size // 2, :]
            encode(mine + precv[2, part(g, d), :], scode.at[2, part(g, d)], mscale.at[g, d])
            for copy in to_relay(g, d):
                copy.start()
        for d in range(2):
            j, p = (1, 3)[d], 1 - d
            mine = pown[j, p * size // 2 : (p + 1) * size // 2, :]
            encode(mine + precv[j, part(g, p), :], scode.at[d, part(g, p)], sscale.at[g, 2 * d + p])
            for copy in to_owner(g, d, p):
                copy.start()
            precv[j, part(g, d), :] = pown[j, d * size // 2 : (d + 1) * size // 2, :] + precv[j, part(g, d), :]
        lad[span(g), :] = pown[0, 0:size, :] + precv[0, span(g), :]

    def relay(g):
        whole(scode.at[2, span(g)], rcode.at[2, span(g)], ms.at[0], mr.at[g]).wait_recv()
        whole(mscale.at[g], nscale.at[g], mss.at[0], msr.at[g]).wait_recv()
        for d in range(2):
            j = (1, 3)[d]
            total = precv[j, part(g, d), :] + decode(rcode.at[2, part(g, d)], nscale.at[g, d])
            encode(total, scode.at[d, part(g, d)], sscale.at[g, 3 * d])
            for copy in to_owner(g, d, d):
                copy.start()

    def direct(e, at):
        zz = (z + STEP[e]) % NZ
        c = at * NK + zz // 4
        rows = pl.ds(pl.multiple_of(at * OT, OT), OT)
        device = {"row": row, "col": c}
        remote = lambda: (
            rc(gsend.at[e, rows], gcode.at[zz % 4, col], gs.at[0], gr.at[zz % 4], device),
            rc(gsendscale.at[e], gscale.at[zz % 4, col], gss.at[0], gsr.at[zz % 4], device),
        )
        local = lambda: (
            pltpu.make_async_copy(gsend.at[e, rows], gcode.at[zz % 4, col], gr.at[zz % 4]),
            pltpu.make_async_copy(gsendscale.at[e], gscale.at[zz % 4, col], gsr.at[zz % 4]),
        )
        return c, remote, local

    def swapped(e, c):
        rows = pl.ds(pl.multiple_of(c * 16, 16), 16)
        device = {"row": across, "col": c}
        return (
            rc(qsend.at[e, rows], qcode.at[e, col], qs.at[0], qr.at[e], device),
            rc(qsendscale.at[e], qscale.at[e, col], qss.at[0], qsr.at[e], device),
        )

    def finish(g):
        others = pl.ds(0, 2)
        whole(scode.at[others, span(g)], rcode.at[others, span(g)], rs.at[0], rr.at[g]).wait_recv()
        whole(sscale.at[g], rscale.at[g], rss.at[0], rsr.at[g]).wait_recv()
        for p in range(2):
            total = lad[part(g, p), :]
            for d in range(2):
                total = total + decode(rcode.at[d, part(g, p)], rscale.at[g, 2 * d + p])
            lad[part(g, p), :] = total
        u = lax.broadcasted_iota(jnp.int32, (TP, TP), 0)
        w = lax.broadcasted_iota(jnp.int32, (TP, TP), 1)
        swap = jnp.where(w == (u % TS) * TS + u // TS, 1.0, 0.0).astype(F32)
        for e in GROUPS[g]:
            value = lad[e * SUB : (e + 1) * SUB, :]
            moved = jnp.dot(value, swap, preferred_element_type=F32, precision=lax.Precision.HIGHEST)
            for half in range(2):
                lanes = slice(half * 128, half * 128 + 128)
                for xx in range(NX):
                    turn[half, pl.ds(xx, OT, stride=NX), :] = moved[xx * OT : (xx + 1) * OT, lanes]
                encode(turn[half], qsend.at[e, :, pl.ds(half * 128, 128)], qsendscale.at[e, :, pl.ds(half * 128, 128)])

            @pl.loop(0, 8)
            def _(c):
                for copy in swapped(e, c):
                    copy.start()

            encode(value, gsend.at[e], gsendscale.at[e])

            @pl.loop(0, NX)
            def _(at):
                c, remote, local = direct(e, at)

                @pl.when(c != col)
                def _():
                    for copy in remote():
                        copy.start()

                @pl.when(c == col)
                def _():
                    for copy in local():
                        copy.start()

    def absorb(g):
        for e in GROUPS[g]:
            zz = (z + STEP[e]) % NZ
            whole(qcode.at[e], qcode.at[e], qs.at[0], qr.at[e]).wait_recv()
            whole(qscale.at[e], qscale.at[e], qss.at[0], qsr.at[e]).wait_recv()

            @pl.loop(0, 8)
            def _(c):
                value = decode(qcode.at[e, c], qscale.at[e, c])
                for half in range(2):
                    acc[half, c, pl.ds(pl.multiple_of(zz * 16, 16), 16), :] = value[:, half * 128 : half * 128 + 128]

    def take_z0(s, h):
        if s < 4:
            both = a[h].at[pl.ds(2 * s - 1, 2), x]
            whole(both, both, z0s.at[h], z0r.at[s - 1, h]).wait_recv()
            for d in range(2):
                if s < 3 or d == h:
                    go(z0(d, s + 1, h))
        else:
            for d in range(2):
                z0(d, 4, d).wait_recv()
        if h == 0:
            for e in (2 * s - 1, 2 * s):
                if e < 8:
                    for d in range(2):
                        go(x0(d, e, False))
            if s == 4:
                go(x2(7, False))

    def take_x1(s):
        for d in range(2):
            x1(d, s, True).wait_recv()
            if s == 1:
                go(x1(d, 2, False))

    def take_x0(e):
        x0(e % 2, e, True).wait_recv()
        if e < 7:
            go(x2(e, False))

    def take_z1(t, s):
        both = a1.at[7, chunk[t]] if s == 4 else a1.at[pl.ds(2 * s - 1, 2), chunk[t]]
        whole(both, both, z1s.at[0], z1r.at[t - 1, s - 1]).wait_recv()
        if s < 4:
            for d in range(2):
                go(z1(t, d, s + 1))

    def start_z1(t):
        for d in range(2):
            go(z1(t, d, 1))

    def ready(g):
        for e in GROUPS[g]:
            x0(1 - e % 2, e, True).wait_recv()
            x2(e, True).wait_recv()

    for d in range(2):
        go(x1(d, 1, False))
    for d in range(2):
        go(z0(d, 1, 0))
    for d in range(2):
        go(x0(d, 0, False))
    mask(0, 2)
    for d in range(2):
        go(z0(d, 1, 1))
    take_z0(1, 0)
    take_x1(1)
    take_z0(1, 1)
    start_z1(1)
    start_z1(2)
    take_x0(0)
    mask(2, 2)
    take_x1(2)
    start_z1(3)
    mask(4, 2)
    take_z0(2, 0)
    take_z0(2, 1)
    take_z1(1, 1)
    take_z1(2, 1)
    take_x0(1)
    take_x0(2)
    take_z1(3, 1)
    mask(6, 2)
    ready(0)
    other_tiles(0)
    own_tiles(0)
    take_z0(3, 0)
    scatter(0)
    take_x0(3)
    take_x0(4)
    take_z0(3, 1)
    take_z1(1, 2)
    take_z1(2, 2)
    take_z1(3, 2)
    ready(1)
    other_tiles(1)
    take_z0(4, 0)
    own_tiles(1)
    relay(0)
    scatter(1)
    take_z1(1, 3)
    take_z1(2, 3)
    take_x0(5)
    take_x0(6)
    take_z1(3, 3)
    ready(2)
    other_tiles(2)
    take_x0(7)
    own_tiles(2)
    scatter(2)
    relay(1)
    take_z1(1, 4)
    take_z1(2, 4)
    take_z1(3, 4)
    ready(3)
    other_tiles(3)
    own_tiles(3)
    scatter(3)
    relay(2)
    ready(4)
    other_tiles(4)
    own_tiles(4)
    scatter(4)
    relay(3)
    finish(0)
    relay(4)
    finish(1)
    finish(2)
    absorb(0)
    finish(3)
    absorb(1)
    finish(4)
    absorb(2)
    absorb(3)
    absorb(4)

    for i in range(4):
        whole(gcode.at[i], gcode.at[i], gs.at[0], gr.at[i]).wait_recv()
        whole(gscale.at[i], gscale.at[i], gss.at[0], gsr.at[i]).wait_recv()

    @pl.loop(0, 8)
    def _(c):
        for i in range(4):
            mine = decode(gcode.at[i, c], gscale.at[i, c])
            for half in range(2):
                theirs = jnp.concatenate([acc[half, c, pl.ds(i * 4 + xx, 8, stride=16), :] for xx in range(NX)], axis=0)
                lanes = pl.ds(pl.multiple_of(c * TP + half * 128, 128), 128)
                out[i * OT : (i + 1) * OT, lanes] = (mine[:, half * 128 : half * 128 + 128] + theirs).astype(BF16)

    def left(ref, sem, rsem):
        whole(ref, ref, sem, rsem).wait_send()

    left(a0.at[pl.ds(0, 7), 0], z0s.at[0], z0r.at[0, 0])
    left(a1.at[pl.ds(0, 7), 0], z0s.at[1], z0r.at[0, 1])
    left(a1.at[0, pl.ds(0, 3)], x1s.at[0], x1r.at[0, 0])
    left(a0.at[:, pl.ds(0, 2)], x0s.at[0], x0r.at[0, 0])
    left(a0.at[:, 0], x2s.at[0], x2r.at[0])
    left(a1.at[pl.ds(0, 7), pl.ds(0, 3)], z1s.at[0], z1r.at[0, 0])
    others = pl.ds(0, 2)
    left(psend, cs.at[0], cr.at[0])
    left(scode.at[others], rs.at[0], rr.at[0])
    left(sscale, rss.at[0], rsr.at[0])
    left(scode.at[2], ms.at[0], mr.at[0])
    left(mscale, mss.at[0], msr.at[0])
    left(gsend.at[pl.ds(0, 7)], gs.at[0], gr.at[0])
    left(gscale.at[:, pl.ds(0, 7)], gss.at[0], gsr.at[0])
    left(qsend, qs.at[0], qr.at[0])
    left(qscale, qss.at[0], qsr.at[0])


def on_device(amplitudes, integrals, tile_irrep, product_pairs, summed_pairs):
    smem = pl.BlockSpec(memory_space=pltpu.SMEM)
    hbm = pl.BlockSpec(memory_space=pl.ANY)
    dma = pltpu.SemaphoreType.DMA
    return pl.pallas_call(
        kernel,
        name="ladder",
        out_shape=jax.ShapeDtypeStruct((128, 2048), BF16),
        in_specs=[smem, smem, smem, hbm, hbm],
        out_specs=pl.BlockSpec(memory_space=pltpu.VMEM),
        scratch_shapes=[
            pltpu.VMEM((8, HALF + REST, TP), BF16),
            pltpu.VMEM((NZ, NX, OT, HALF), BF16),
            pltpu.VMEM((NZ, NX, OT, REST), BF16),
            pltpu.VMEM((NY, OT * OT, TP), F32),
            pltpu.VMEM((NY, 2 * SUB, TP), F32),
            pltpu.VMEM((NY, OT * OT, TP), F32),
            pltpu.VMEM((NY, OT * OT, TP), I16),
            pltpu.VMEM((5, NY, 1, TP), F32),
            pltpu.VMEM((NY, OT * OT, TP), I16),
            pltpu.VMEM((5, NY, 1, TP), F32),
            pltpu.VMEM((5, 2, 1, TP), F32),
            pltpu.VMEM((5, 2, 1, TP), F32),
            pltpu.VMEM((OT * OT, TP), F32),
            pltpu.VMEM((8, SUB, TP), I16),
            pltpu.VMEM((8, 1, TP), F32),
            pltpu.VMEM((4, 8, OT, TP), I16),
            pltpu.VMEM((4, 8, 1, TP), F32),
            pltpu.VMEM((8, SUB, TP), I16),
            pltpu.VMEM((8, 1, TP), F32),
            pltpu.VMEM((8, 8, 16, TP), I16),
            pltpu.VMEM((8, 8, 1, TP), F32),
            pltpu.VMEM((2, SUB, 128), F32),
            pltpu.VMEM((2, 8, SUB, 128), F32),
            dma((2,)), dma((8,)),
            dma((2,)), dma((4, 2)),
            dma((1,)), dma((2, 2)),
            dma((1,)), dma((2, 8)),
            dma((1,)), dma((8,)),
            dma((1,)), dma((3, 4)),
            dma((1,)), dma((5,)),
            dma((1,)), dma((5,)), dma((1,)), dma((5,)),
            dma((1,)), dma((5,)), dma((1,)), dma((5,)),
            dma((1,)), dma((4,)), dma((1,)), dma((4,)),
            dma((1,)), dma((8,)), dma((1,)), dma((8,)),
        ],
        compiler_params=pltpu.CompilerParams(collective_id=0, has_side_effects=True, vmem_limit_bytes=56 << 20),
    )(tile_irrep, product_pairs.T, summed_pairs.T, amplitudes, integrals)


def solution(mesh):
    return jax.shard_map(
        on_device,
        mesh=mesh,
        in_specs=(P("row", "col"), P("col", "row"), P(), P("row", None), P("col", None)),
        out_specs=P("col", "row"),
        check_vma=False,
    )
```
